32 devices in a mesh: fsdp: 4 (over x, core), ctx: 8 (over z, y).
Axes of the slice: x: 2, y: 2, z: 4, core: 2. Of those that a mesh axis runs over, the one named last changes fastest.
Arguments:
- layer_in: bfloat16 [8, 4, 128, 1024], P('ctx', 'fsdp'), may hold values from -6 to 6
- grad_out: bfloat16 [8, 4, 128, 1024], P('ctx', 'fsdp'), may hold values from -6 to 6
- pair_of_rank: int32 [8], replicated, may hold values from 0 to 7, each once
- ln1_gain: bfloat16 [1024], P(('fsdp', 'ctx')), may hold values from 0.5 to 1.5
- ln1_bias: bfloat16 [1024], P(('fsdp', 'ctx')), may hold values from -1.5 to 1.5
- ln2_gain: bfloat16 [1024], P(('fsdp', 'ctx')), may hold values from 0.5 to 1.5
- ln2_bias: bfloat16 [1024], P(('fsdp', 'ctx')), may hold values from -1.5 to 1.5
- w_qkv: bfloat16 [1024, 3072], P(('fsdp', 'ctx')), may hold values from -4 to 4
- b_qkv: bfloat16 [3072], P(('fsdp', 'ctx')), may hold values from -2.5 to 2.5
- w_out: bfloat16 [1024, 1024], P(('fsdp', 'ctx')), may hold values from -3 to 3
- b_out: bfloat16 [1024], P(('fsdp', 'ctx')), may hold values from -2.5 to 2.5
- w_up: bfloat16 [1024, 4096], P(('fsdp', 'ctx')), may hold values from -0.1875 to 0.1875
- b_up: bfloat16 [4096], P(('fsdp', 'ctx')), may hold values from -2.5 to 2.5
- w_down: bfloat16 [1024, 4096], P(('fsdp', 'ctx')), may hold values from -0.09375 to 0.09375
- b_down: bfloat16 [1024], P(('fsdp', 'ctx')), may hold values from -2.5 to 2.5
Outputs:
- layer_out: bfloat16 [8, 4, 128, 1024], P('ctx', 'fsdp')
- grad_x: bfloat16 [8, 4, 128, 1024], P('ctx', 'fsdp')
- grad_ln1_gain: float32 [1024], P(('fsdp', 'ctx'))
- grad_ln1_bias: float32 [1024], P(('fsdp', 'ctx'))
- grad_ln2_gain: float32 [1024], P(('fsdp', 'ctx'))
- grad_ln2_bias: float32 [1024], P(('fsdp', 'ctx'))
- grad_w_qkv: float32 [1024, 3072], P(('fsdp', 'ctx'))
- grad_b_qkv: float32 [3072], P(('fsdp', 'ctx'))
- grad_w_out: float32 [1024, 1024], P(('fsdp', 'ctx'))
- grad_b_out: float32 [1024], P(('fsdp', 'ctx'))
- grad_w_up: float32 [1024, 4096], P(('fsdp', 'ctx'))
- grad_b_up: float32 [4096], P(('fsdp', 'ctx'))
- grad_w_down: float32 [1024, 4096], P(('fsdp', 'ctx'))
- grad_b_down: float32 [1024], P(('fsdp', 'ctx'))
The draws below stay inside these ranges and needn't reach their ends.
Inputs may be any that keep to these rules, and one draw needn't show every extreme that they name: `pair_of_rank`: a permutation: each slot holds a different block pair, so block pairs 0 to 7 each appear once.
All inputs are finite; a program needn't handle non-finite values.
Results may differ from the reference program's by a relative error of at most 0.011.
Values may be sent and summed in bfloat16 or wider, within the bound.
A program may use at most 512 MiB of HBM per device.

```python
import math
import jax
import jax.numpy as jnp
from jax import lax

D = 1024
H = 16
HD = 64
FF = 4096
ROT = 16
BLK = 64
BATCH = 4
N_CTX = 8


def draw_w_qkv(key, part):
    base = jax.random.normal(key, (D, 3 * D), jnp.float32) / math.sqrt(D)
    return base.astype(jnp.bfloat16)


def raised(values, stream_key, source, target, parts, factor):
    def block_of(position):
        return (jnp.arange(values.shape[position]) // (values.shape[position] // parts)).reshape((-1,) + (1,) * (values.ndim - 1 - position))

    one_side = jax.random.permutation(stream_key, parts)[block_of(target)]
    second = (block_of(target) + parts // 2) % parts
    return jnp.where((block_of(source) == one_side) | (block_of(source) == second), factor * values, values)


def shard_levels(rng, shape, shards, low, high):
    def one(dim, blocks):
        draws = jax.random.uniform(jax.random.fold_in(jax.random.fold_in(rng, 6), dim), (blocks,), jnp.float32, low / len(shards), high / len(shards))
        return jnp.repeat(jnp.exp(draws), shape[dim] // blocks).reshape((-1,) + (1,) * (len(shape) - dim - 1))

    loudness = one(*shards[0])
    for cut in shards[1:]:
        loudness = loudness * one(*cut)
    return loudness


def scatter_about(rng, shape, spread, bound, split=(), kind=jnp.bfloat16):
    entries = spread * jax.random.normal(rng, shape, jnp.float32)
    if split:
        entries = entries * shard_levels(rng, shape, split, -0.22, 0.18)
    return jnp.clip(entries, -bound, bound).astype(kind)


def heavy_noise(own_key, extent, spread, most, shards, heavy, held_as=jnp.bfloat16):
    values = spread * jax.random.normal(own_key, extent, jnp.float32)
    if shards:
        values = values * shard_levels(own_key, extent, shards, -0.22, 0.18)
    return jnp.clip(raised(values, jax.random.fold_in(own_key, 3), *heavy), -most, most).astype(held_as)


def setup_inputs(seed: int = 0) -> dict:
    seeds = jax.random.split(jax.random.key(seed), 16)
    return {
        "layer_in": scatter_about(seeds[0], (N_CTX, BATCH, 2 * BLK, D), 1.0, 6.0, ((0, 8), (1, 4))),
        "grad_out": heavy_noise(seeds[1], (N_CTX, BATCH, 2 * BLK, D), 1.0, 6.0, ((0, 8), (1, 4)), (0, 3, 8, 2.0)),
        "pair_of_rank": jax.random.permutation(seeds[2], N_CTX).astype(jnp.int32),
        "ln1_gain": jnp.clip(1.0 + 0.1 * jax.random.normal(seeds[3], (D,), jnp.float32), 0.5, 1.5).astype(jnp.bfloat16),
        "ln1_bias": scatter_about(seeds[4], (D,), 0.3, 1.5, ((0, 32),)),
        "ln2_gain": jnp.clip(1.0 + 0.1 * jax.random.normal(seeds[5], (D,), jnp.float32), 0.5, 1.5).astype(jnp.bfloat16),
        "ln2_bias": scatter_about(seeds[6], (D,), 0.3, 1.5, ((0, 32),)),
        "w_qkv": draw_w_qkv(jax.random.fold_in(seeds[15], 71), 0),
        "b_qkv": scatter_about(seeds[8], (3 * D,), 0.5, 2.5, ((0, 32),)),
        "w_out": scatter_about(seeds[9], (D, D), (max(D // 256, 1)) ** -0.5, 3.0, ((0, 32),)),
        "b_out": scatter_about(seeds[10], (D,), 0.5, 2.5, ((0, 32),)),
        "w_up": scatter_about(seeds[11], (D, FF), D ** -0.5, 0.1875, ((0, 32),)),
        "b_up": scatter_about(seeds[12], (FF,), 0.5, 2.5, ((0, 32),)),
        "w_down": scatter_about(seeds[13], (D, FF), FF ** -0.5, 0.09375, ((0, 32),)),
        "b_down": scatter_about(seeds[14], (D,), 0.5, 2.5, ((0, 32),)),
    }


EPS = 1e-05
NEG = -1e+30
ROOT_HALF = 0.7071067811865476
INV_ROOT_TAU = 0.3989422804014327

def norm_parts(xf, scale_weight, shift_bias):
    row_mean = lax.optimization_barrier(jnp.mean(xf, axis=-1, keepdims=True))
    centred_input = xf - row_mean
    inverse_deviation = lax.rsqrt(lax.optimization_barrier(jnp.mean(centred_input * centred_input, axis=-1, keepdims=True)) + EPS)
    normalized_input = centred_input * inverse_deviation
    return (normalized_input * scale_weight.astype(jnp.float32) + shift_bias.astype(jnp.float32), normalized_input, inverse_deviation)

def layer_norm_backward(norm_output_gradient, normalized_input, inverse_deviation, scale_weight):
    normalized_gradient = norm_output_gradient * scale_weight.astype(jnp.float32)
    return inverse_deviation * (normalized_gradient - lax.optimization_barrier(jnp.mean(normalized_gradient, axis=-1, keepdims=True)) - normalized_input * lax.optimization_barrier(jnp.mean(normalized_gradient * normalized_input, axis=-1, keepdims=True)))

def gelu_value(u):
    return 0.5 * u * (1.0 + lax.erf(u * ROOT_HALF))

def gelu_slope(u):
    return 0.5 * (1.0 + lax.erf(u * ROOT_HALF)) + u * jnp.exp(-0.5 * u * u) * INV_ROOT_TAU

def rotate(field, place, sign):
    half = ROT // 2
    freqs = jnp.exp(jnp.arange(half).astype(jnp.float32) * (-2.0 * math.log(10000.0) / ROT))
    angle = place.astype(jnp.float32)[..., None] * freqs
    cosine = jnp.cos(angle)[..., None, :]
    sine = sign * jnp.sin(angle)[..., None, :]
    first = field[..., :half]
    second = field[..., half:ROT]
    return jnp.concatenate([first * cosine - second * sine, second * cosine + first * sine, field[..., ROT:]], axis=-1)

def slot_places(pairs):
    offsets = jnp.arange(BLK, dtype=jnp.int32)
    early = pairs[:, None] * BLK + offsets[None, :]
    late = (2 * N_CTX - 1 - pairs)[:, None] * BLK + offsets[None, :]
    return jnp.concatenate([early, late], axis=1).astype(jnp.int32)

def reference(layer_in, grad_out, pair_of_rank, ln1_gain, ln1_bias, ln2_gain, ln2_bias, w_qkv, b_qkv, w_out, b_out, w_up, b_up, w_down, b_down):
    f32 = jnp.float32
    bf = jnp.bfloat16
    length = 2 * BLK * N_CTX
    scale = 1.0 / math.sqrt(HD)
    places = slot_places(pair_of_rank).reshape(length)
    qblock = 512 if length % 512 == 0 else length
    nblocks = length // qblock
    pblocks = places.reshape(nblocks, qblock)

    def one_sequence(grads, inputs):
        xs, gs = inputs
        xf = xs.reshape(length, D).astype(f32)
        norm1, hat1, rstd1 = norm_parts(xf, ln1_gain, ln1_bias)
        norm2, hat2, rstd2 = norm_parts(xf, ln2_gain, ln2_bias)
        norm1 = norm1.astype(bf)
        norm2 = norm2.astype(bf)
        qkv = jnp.dot(norm1, w_qkv, preferred_element_type=f32) + b_qkv.astype(f32)
        query = rotate(qkv[:, :D].reshape(length, H, HD), places, 1.0).astype(bf)
        key = rotate(qkv[:, D:2 * D].reshape(length, H, HD), places, 1.0).astype(bf)
        value = qkv[:, 2 * D:].reshape(length, H, HD).astype(bf)
        keyf = key.astype(f32)
        valuef = value.astype(f32)
        qblocks = query.reshape(nblocks, qblock, H, HD)

        def attend(args):
            qpart, qplace = args
            visible = places[None, None, :] <= qplace[None, :, None]
            score = jnp.einsum('qhd,khd->hqk', qpart.astype(f32), keyf) * scale
            score = jnp.where(visible, score, NEG)
            top = lax.optimization_barrier(jnp.max(score, axis=-1))
            weight = jnp.where(visible, jnp.exp(score - top[..., None]), 0.0)
            total = lax.optimization_barrier(jnp.sum(weight, axis=-1))
            mixed = jnp.einsum('hqk,khd->hqd', weight.astype(bf).astype(f32), valuef)
            return ((mixed / total[..., None]).transpose(1, 0, 2), (top + jnp.log(total)).T)
        ctx_blocks, lse_blocks = lax.map(attend, (qblocks, pblocks))
        context = ctx_blocks.reshape(length, D).astype(bf)
        lse = lse_blocks.reshape(length, H)
        attn = jnp.dot(context, w_out, preferred_element_type=f32) + b_out.astype(f32)
        pre = jnp.dot(norm2, w_up, preferred_element_type=f32) + b_up.astype(f32)
        hidden = gelu_value(pre).astype(bf)
        mlp = jnp.dot(hidden, w_down.T, preferred_element_type=f32) + b_down.astype(f32)
        out = (xf + attn + mlp).astype(bf)
        grad_b = gs.reshape(length, D)
        grad_f = grad_b.astype(f32)
        dhidden = jnp.dot(grad_b, w_down, preferred_element_type=f32)
        dpre = dhidden * gelu_slope(pre)
        dpre_b = dpre.astype(bf)
        dnorm2 = jnp.dot(dpre_b, w_up.T, preferred_element_type=f32)
        dcontext = jnp.dot(grad_b, w_out.T, preferred_element_type=f32).astype(bf)
        dctx3 = dcontext.reshape(length, H, HD)
        delta = lax.optimization_barrier(jnp.sum(dctx3.astype(f32) * context.reshape(length, H, HD).astype(f32), axis=-1))

        def back(carry, args):
            dkey, dvalue = carry
            qpart, dpart, lpart, delpart, qplace = args
            visible = places[None, None, :] <= qplace[None, :, None]
            score = jnp.einsum('qhd,khd->hqk', qpart.astype(f32), keyf) * scale
            score = jnp.where(visible, score, NEG)
            prob = jnp.where(visible, jnp.exp(score - lpart.T[..., None]), 0.0)
            dvalue = dvalue + jnp.einsum('hqk,qhd->khd', prob.astype(bf).astype(f32), dpart.astype(f32))
            dprob = jnp.einsum('qhd,khd->hqk', dpart.astype(f32), valuef)
            dscore = (scale * prob * (dprob - delpart.T[..., None])).astype(bf).astype(f32)
            dquery = jnp.einsum('hqk,khd->qhd', dscore, keyf)
            dkey = dkey + jnp.einsum('hqk,qhd->khd', dscore, qpart.astype(f32))
            return ((dkey, dvalue), dquery)
        zero = jnp.zeros((length, H, HD), f32)
        (dkey, dvalue), dquery = lax.scan(back, (zero, zero), (qblocks, dctx3.reshape(nblocks, qblock, H, HD), lse.reshape(nblocks, qblock, H), delta.reshape(nblocks, qblock, H), pblocks))
        dquery = dquery.reshape(length, H, HD)
        dqkv = jnp.concatenate([rotate(dquery, places, -1.0).reshape(length, D), rotate(dkey, places, -1.0).reshape(length, D), dvalue.reshape(length, D)], axis=1)
        dqkv_b = dqkv.astype(bf)
        dnorm1 = jnp.dot(dqkv_b, w_qkv.T, preferred_element_type=f32)
        dx = (grad_f + layer_norm_backward(dnorm1, hat1, rstd1, ln1_gain) + layer_norm_backward(dnorm2, hat2, rstd2, ln2_gain)).astype(bf)
        new = (grads[0] + lax.optimization_barrier(jnp.sum(dnorm1 * hat1, axis=0)), grads[1] + lax.optimization_barrier(jnp.sum(dnorm1, axis=0)), grads[2] + lax.optimization_barrier(jnp.sum(dnorm2 * hat2, axis=0)), grads[3] + lax.optimization_barrier(jnp.sum(dnorm2, axis=0)), grads[4] + jnp.dot(norm1.T, dqkv_b, preferred_element_type=f32), grads[5] + lax.optimization_barrier(jnp.sum(dqkv, axis=0)), grads[6] + jnp.dot(context.T, grad_b, preferred_element_type=f32), grads[7] + lax.optimization_barrier(jnp.sum(grad_f, axis=0)), grads[8] + jnp.dot(norm2.T, dpre_b, preferred_element_type=f32), grads[9] + lax.optimization_barrier(jnp.sum(dpre, axis=0)), grads[10] + jnp.dot(grad_b.T, hidden, preferred_element_type=f32))
        return (new, (out.reshape(N_CTX, 2 * BLK, D), dx.reshape(N_CTX, 2 * BLK, D)))
    start = (jnp.zeros((D,), f32), jnp.zeros((D,), f32), jnp.zeros((D,), f32), jnp.zeros((D,), f32), jnp.zeros((D, 3 * D), f32), jnp.zeros((3 * D,), f32), jnp.zeros((D, D), f32), jnp.zeros((D,), f32), jnp.zeros((D, FF), f32), jnp.zeros((FF,), f32), jnp.zeros((D, FF), f32))
    grads, (outs, dxs) = lax.scan(one_sequence, start, (layer_in.transpose(1, 0, 2, 3), grad_out.transpose(1, 0, 2, 3)))
    layer_out = outs.transpose(1, 0, 2, 3)
    grad_x = dxs.transpose(1, 0, 2, 3)
    return (layer_out, grad_x, grads[0], grads[1], grads[2], grads[3], grads[4], grads[5], grads[6], grads[7], grads[8], grads[9], grads[10], grads[7])
```

```python
import math

import jax
import jax.numpy as jnp
from jax import lax
from jax.sharding import PartitionSpec as P

HD = 64
ROT = 16


EPS = 1e-05
NEG = -1e30
ROOT_HALF = 0.7071067811865476
INV_ROOT_TAU = 0.3989422804014327


def norm_parts(xf, scale_weight, shift_bias):
    row_mean = jnp.mean(xf, axis=-1, keepdims=True)
    centred_input = xf - row_mean
    inverse_deviation = lax.rsqrt(
        jnp.mean(centred_input * centred_input, axis=-1, keepdims=True) + EPS
    )
    normalized_input = centred_input * inverse_deviation
    return (
        normalized_input * scale_weight.astype(jnp.float32) + shift_bias.astype(jnp.float32),
        normalized_input,
        inverse_deviation,
    )


def layer_norm_backward(norm_output_gradient, normalized_input, inverse_deviation, scale_weight):
    normalized_gradient = norm_output_gradient * scale_weight.astype(jnp.float32)
    return inverse_deviation * (
        normalized_gradient
        - jnp.mean(normalized_gradient, axis=-1, keepdims=True)
        - normalized_input
        * jnp.mean(normalized_gradient * normalized_input, axis=-1, keepdims=True)
    )


def gelu_value(u):
    return 0.5 * u * (1.0 + lax.erf(u * ROOT_HALF))


def gelu_slope(u):
    return 0.5 * (1.0 + lax.erf(u * ROOT_HALF)) + u * jnp.exp(-0.5 * u * u) * INV_ROOT_TAU


def rotate(field, place, sign):
    half = ROT // 2
    freqs = jnp.exp(jnp.arange(half).astype(jnp.float32) * (-2.0 * math.log(10000.0) / ROT))
    angle = place.astype(jnp.float32)[..., None] * freqs
    cosine = jnp.cos(angle)[..., None, :]
    sine = sign * jnp.sin(angle)[..., None, :]
    first = field[..., :half]
    second = field[..., half:ROT]
    return jnp.concatenate(
        [first * cosine - second * sine, second * cosine + first * sine, field[..., rot_end() :]],
        axis=-1,
    )


def rot_end():
    return ROT


def leading(field, letters):
    return "n" + letters if field.ndim == 5 else letters


def product(left, left_letters, right, right_letters, result):
    form = leading(left, left_letters) + "," + leading(right, right_letters) + "->" + result
    return jnp.einsum(form, left, right, preferred_element_type=jnp.float32)


def selectors(sel):
    return (sel[:, None, None, None, None], sel[:, None, None, None], sel[:, None])


def visibility(sel, qpa, qpb, kpa, kpb):
    chosen = sel[:, None]
    key_place = jnp.where(chosen, kpa, kpb)
    query_place = jnp.where(chosen, qpa, qpb)
    return (key_place[:, None, :] <= query_place[:, :, None])[:, None, None]


def online_update(state, qa, qb, ka, kb, va, vb, qpa, qpb, kpa, kpb, sel, with_first, scale):
    top_a, total_a, acc_a, top_b, total_b, acc_b = state
    sel5, sel4, sel2 = selectors(sel)
    query_two = jnp.where(sel5, qa, qb)
    key_two = jnp.where(sel5, ka, kb)
    value_two = jnp.where(sel5, va, vb)
    visible = visibility(sel, qpa, qpb, kpa, kpb)
    score = jnp.where(visible, product(query_two, "sqhd", key_two, "skhd", "nshqk") * scale, NEG)
    peak_a = jnp.max(jnp.where(sel5, score, NEG), axis=(0, 4))
    peak_b = jnp.max(jnp.where(sel5, NEG, score), axis=(0, 4))
    if with_first:
        score_one = product(qb, "sqhd", ka, "skhd", "nshqk") * scale
        peak_b = jnp.maximum(peak_b, jnp.max(score_one, axis=(0, 4)))
    new_a = jnp.maximum(top_a, peak_a)
    new_b = jnp.maximum(top_b, peak_b)
    lifted = jnp.where(sel5, new_a[..., None], new_b[..., None])
    weight = jnp.where(visible, jnp.exp(score - lifted), 0.0)
    mixed = product(weight.astype(jnp.bfloat16), "shqk", value_two, "skhd", "nshqd")
    mass = jnp.sum(weight, axis=4)
    add_total_a = jnp.sum(jnp.where(sel4, mass, 0.0), axis=0)
    add_total_b = jnp.sum(jnp.where(sel4, 0.0, mass), axis=0)
    add_acc_a = jnp.sum(jnp.where(sel5, mixed, 0.0), axis=0)
    add_acc_b = jnp.sum(jnp.where(sel5, 0.0, mixed), axis=0)
    if with_first:
        weight_one = jnp.exp(score_one - new_b[..., None])
        add_total_b = add_total_b + jnp.sum(weight_one, axis=(0, 4))
        add_acc_b = add_acc_b + product(weight_one.astype(jnp.bfloat16), "shqk", va, "skhd", "shqd")
    decay_a = jnp.exp(top_a - new_a)
    decay_b = jnp.exp(top_b - new_b)
    return (
        new_a,
        total_a * decay_a + add_total_a,
        acc_a * decay_a[..., None] + add_acc_a,
        new_b,
        total_b * decay_b + add_total_b,
        acc_b * decay_b[..., None] + add_acc_b,
    )


def pair_terms(
    qa,
    qb,
    ka,
    kb,
    va,
    vb,
    da,
    db,
    lsea,
    lseb,
    dela,
    delb,
    qpa,
    qpb,
    kpa,
    kpb,
    sel,
    with_first,
    scale,
):
    sel5, sel4, sel2 = selectors(sel)
    query_two = jnp.where(sel5, qa, qb)
    key_two = jnp.where(sel5, ka, kb)
    value_two = jnp.where(sel5, va, vb)
    dctx_two = jnp.where(sel5, da, db)
    lse_two = jnp.where(sel4, lsea, lseb)
    delta_two = jnp.where(sel4, dela, delb)
    visible = visibility(sel, qpa, qpb, kpa, kpb)
    score = jnp.where(visible, product(query_two, "sqhd", key_two, "skhd", "nshqk") * scale, NEG)
    prob = jnp.exp(score - lse_two[..., None])
    dprob = product(dctx_two, "sqhd", value_two, "skhd", "nshqk")
    dscore = (scale * prob * (dprob - delta_two[..., None])).astype(jnp.bfloat16)
    first_ds = None
    first_prob = None
    if with_first:
        score_one = product(qb, "sqhd", ka, "skhd", "nshqk") * scale
        prob_one = jnp.exp(score_one - lseb[..., None])
        dprob_one = product(db, "sqhd", va, "skhd", "nshqk")
        first_ds = (scale * prob_one * (dprob_one - delb[..., None])).astype(jnp.bfloat16)
        first_prob = prob_one.astype(jnp.bfloat16)
    return (first_ds, first_prob, dscore, prob.astype(jnp.bfloat16))


def query_grads(terms, ka, kb, sel):
    sel5, sel4, sel2 = selectors(sel)
    key_two = jnp.where(sel5, ka, kb)
    dq_two = product(terms[2], "shqk", key_two, "skhd", "nsqhd")
    dq_a = jnp.where(sel5, dq_two, 0.0)
    dq_b = jnp.where(sel5, 0.0, dq_two)
    if terms[0] is not None:
        dq_b = dq_b + product(terms[0], "shqk", ka, "skhd", "nsqhd")
    return (dq_a, dq_b)


def key_grads(terms, qa, qb, da, db, sel):
    sel5, sel4, sel2 = selectors(sel)
    query_two = jnp.where(sel5, qa, qb)
    dctx_two = jnp.where(sel5, da, db)
    dk_two = product(terms[2], "shqk", query_two, "sqhd", "nskhd")
    dv_two = product(terms[3], "shqk", dctx_two, "sqhd", "nskhd")
    dk_a = jnp.where(sel5, dk_two, 0.0)
    dk_b = jnp.where(sel5, 0.0, dk_two)
    dv_a = jnp.where(sel5, dv_two, 0.0)
    dv_b = jnp.where(sel5, 0.0, dv_two)
    if terms[0] is not None:
        dk_a = dk_a + product(terms[0], "shqk", qb, "sqhd", "nskhd")
        dv_a = dv_a + product(terms[1], "shqk", db, "sqhd", "nskhd")
    return (dk_a, dk_b, dv_a, dv_b)


def tdot(left, right):
    return lax.dot_general(
        left, right, (((0,), (0,)), ((), ())), preferred_element_type=jnp.float32
    )


def rdot(left, right):
    return lax.dot_general(
        left, right, (((1,), (1,)), ((), ())), preferred_element_type=jnp.float32
    )


def shards(
    layer_in,
    grad_out,
    pair_of_rank,
    ln1_gain,
    ln1_bias,
    ln2_gain,
    ln2_bias,
    w_qkv,
    b_qkv,
    w_out,
    b_out,
    w_up,
    b_up,
    w_down,
    b_down,
):
    f32 = jnp.float32
    bf = jnp.bfloat16
    nctx = lax.axis_size("ctx")
    mine = pair_of_rank[lax.axis_index("ctx")]
    seqs = layer_in.shape[1]
    width2 = layer_in.shape[2]
    dmodel = layer_in.shape[3]
    blk = width2 // 2
    rows = seqs * width2
    heads = dmodel // HD
    scale = 1.0 / math.sqrt(HD)
    offsets = jnp.arange(blk, dtype=jnp.int32)
    place_a = mine * blk + offsets
    place_b = (2 * nctx - 1 - mine) * blk + offsets
    places = jnp.concatenate([place_a, place_b])
    params = (
        ln1_gain,
        ln1_bias,
        ln2_gain,
        ln2_bias,
        w_qkv,
        b_qkv,
        w_out,
        b_out,
        w_up,
        b_up,
        w_down,
        b_down,
    )
    full = (
        lax.all_gather(params[0], ("fsdp", "ctx"), axis=0, tiled=True),
        lax.all_gather(params[1], ("fsdp", "ctx"), axis=0, tiled=True),
        lax.all_gather(params[2], ("fsdp", "ctx"), axis=0, tiled=True),
        lax.all_gather(params[3], ("fsdp", "ctx"), axis=0, tiled=True),
        lax.all_gather(params[4], ("fsdp", "ctx"), axis=0, tiled=True),
        lax.all_gather(params[5], ("fsdp", "ctx"), axis=0, tiled=True),
        lax.all_gather(params[6], ("fsdp", "ctx"), axis=0, tiled=True),
        lax.all_gather(params[7], ("fsdp", "ctx"), axis=0, tiled=True),
        lax.all_gather(params[8], ("fsdp", "ctx"), axis=0, tiled=True),
        lax.all_gather(params[9], ("fsdp", "ctx"), axis=0, tiled=True),
        lax.all_gather(params[10], ("fsdp", "ctx"), axis=0, tiled=True),
        lax.all_gather(params[11], ("fsdp", "ctx"), axis=0, tiled=True),
    )
    xf = layer_in.reshape(rows, dmodel).astype(f32)
    norm1, hat1, rstd1 = norm_parts(xf, full[0], full[1])
    norm2, hat2, rstd2 = norm_parts(xf, full[2], full[3])
    norm1 = norm1.astype(bf)
    norm2 = norm2.astype(bf)
    qkv = jnp.dot(norm1, full[4], preferred_element_type=f32) + full[5].astype(f32)
    query = rotate(qkv[:, :dmodel].reshape(seqs, width2, heads, HD), places, 1.0).astype(bf)
    key = rotate(qkv[:, dmodel : 2 * dmodel].reshape(seqs, width2, heads, HD), places, 1.0).astype(
        bf
    )
    value = qkv[:, 2 * dmodel :].reshape(seqs, width2, heads, HD).astype(bf)
    query_a = query[:, :blk]
    query_b = query[:, blk:]
    key_b = key[:, blk:]
    value_b = value[:, blk:]
    lone = jnp.zeros((1,), dtype=bool)
    empty_top = jnp.full((seqs, heads, blk), NEG, f32)
    empty_total = jnp.zeros((seqs, heads, blk), f32)
    empty_acc = jnp.zeros((seqs, heads, blk, HD), f32)
    state = (empty_top, empty_total, empty_acc, empty_top, empty_total, empty_acc)
    state = online_update(
        state,
        query_a,
        query_b,
        key_b[None],
        key_b[None],
        value_b[None],
        value_b[None],
        place_a,
        place_b,
        place_b[None],
        place_b[None],
        lone,
        False,
        scale,
    )

    def key_parts(kpiece, vpiece, first):
        count = kpiece.shape[0]
        pairs = lax.dynamic_slice_in_dim(pair_of_rank, first, count)
        keys = kpiece.reshape(count, seqs, width2, heads, HD)
        values = vpiece.reshape(count, seqs, width2, heads, HD)
        kplace_a = pairs[:, None] * blk + offsets[None, :]
        kplace_b = (2 * nctx - 1 - pairs)[:, None] * blk + offsets[None, :]
        return (
            keys[:, :, :blk],
            keys[:, :, blk:],
            values[:, :, :blk],
            values[:, :, blk:],
            kplace_a,
            kplace_b,
            pairs,
        )

    key_send = key.reshape(1, seqs, width2, dmodel)
    value_send = value.reshape(1, seqs, width2, dmodel)
    ka, kb, va, vb, kpa, kpb, pairs = key_parts(
        lax.all_gather(key_send, "ctx", axis=0, tiled=True),
        lax.all_gather(value_send, "ctx", axis=0, tiled=True),
        jnp.int32(0),
    )
    state = online_update(
        state,
        query_a,
        query_b,
        ka,
        kb,
        va,
        vb,
        place_a,
        place_b,
        kpa,
        kpb,
        pairs <= mine,
        True,
        scale,
    )
    top_a, total_a, acc_a, top_b, total_b, acc_b = state
    context4 = jnp.concatenate([acc_a / total_a[..., None], acc_b / total_b[..., None]], axis=2)
    lse = jnp.concatenate([top_a + jnp.log(total_a), top_b + jnp.log(total_b)], axis=2)
    context = context4.transpose(0, 2, 1, 3).reshape(rows, dmodel).astype(bf)
    attn = jnp.dot(context, full[6], preferred_element_type=f32) + full[7].astype(f32)
    pre = jnp.dot(norm2, full[8], preferred_element_type=f32) + full[9].astype(f32)
    hidden = gelu_value(pre).astype(bf)
    mlp = rdot(hidden, full[10]) + full[11].astype(f32)
    layer_out = (xf + attn + mlp).astype(bf).reshape(layer_in.shape)
    again = (
        lax.all_gather(params[0], ("fsdp", "ctx"), axis=0, tiled=True),
        lax.all_gather(params[1], ("fsdp", "ctx"), axis=0, tiled=True),
        lax.all_gather(params[2], ("fsdp", "ctx"), axis=0, tiled=True),
        lax.all_gather(params[3], ("fsdp", "ctx"), axis=0, tiled=True),
        lax.all_gather(params[4], ("fsdp", "ctx"), axis=0, tiled=True),
        lax.all_gather(params[5], ("fsdp", "ctx"), axis=0, tiled=True),
        lax.all_gather(params[6], ("fsdp", "ctx"), axis=0, tiled=True),
        lax.all_gather(params[7], ("fsdp", "ctx"), axis=0, tiled=True),
        lax.all_gather(params[8], ("fsdp", "ctx"), axis=0, tiled=True),
        lax.all_gather(params[9], ("fsdp", "ctx"), axis=0, tiled=True),
        lax.all_gather(params[10], ("fsdp", "ctx"), axis=0, tiled=True),
        lax.all_gather(params[11], ("fsdp", "ctx"), axis=0, tiled=True),
    )
    grad_b = grad_out.reshape(rows, dmodel)
    grad_f = grad_b.astype(f32)
    dhidden = jnp.dot(grad_b, again[10], preferred_element_type=f32)
    dpre = dhidden * gelu_slope(pre)
    dpre_b = dpre.astype(bf)
    dnorm2 = rdot(dpre_b, again[8])
    dcontext = rdot(grad_b, again[6]).astype(bf)
    dctx4 = dcontext.reshape(seqs, width2, heads, HD)
    delta = jnp.sum(
        dctx4.astype(f32) * context.reshape(seqs, width2, heads, HD).astype(f32), axis=-1
    ).transpose(0, 2, 1)
    dctx_a = dctx4[:, :blk]
    dctx_b = dctx4[:, blk:]
    lse_a = lse[..., :blk]
    lse_b = lse[..., blk:]
    delta_a = delta[..., :blk]
    delta_b = delta[..., blk:]
    own = pair_terms(
        query_b,
        query_b,
        key_b[None],
        key_b[None],
        value_b[None],
        value_b[None],
        dctx_b,
        dctx_b,
        lse_b,
        lse_b,
        delta_b,
        delta_b,
        place_b,
        place_b,
        place_b[None],
        place_b[None],
        lone,
        False,
        scale,
    )
    own_dq = query_grads(own, key_b[None], key_b[None], lone)[1][0]
    own_keys = key_grads(own, query_b, query_b, dctx_b, dctx_b, lone)
    gathered = (
        lax.all_gather(key_send, "ctx", axis=0, tiled=True),
        lax.all_gather(value_send, "ctx", axis=0, tiled=True),
    )
    groups = math.gcd(nctx, 8)
    per = nctx // groups

    def group_terms(args):
        kpiece, vpiece, first = args
        ka, kb, va, vb, kpa, kpb, pairs = key_parts(kpiece, vpiece, first)
        sel = pairs <= mine
        terms = pair_terms(
            query_a,
            query_b,
            ka,
            kb,
            va,
            vb,
            dctx_a,
            dctx_b,
            lse_a,
            lse_b,
            delta_a,
            delta_b,
            place_a,
            place_b,
            kpa,
            kpb,
            sel,
            True,
            scale,
        )
        dq_a, dq_b = query_grads(terms, ka, kb, sel)
        return (terms, jnp.sum(dq_a, axis=0), jnp.sum(dq_b, axis=0))

    grouped = lax.map(
        group_terms,
        (
            gathered[0].reshape(groups, per, seqs, width2, dmodel),
            gathered[1].reshape(groups, per, seqs, width2, dmodel),
            jnp.arange(groups, dtype=jnp.int32) * per,
        ),
    )
    terms_all = tuple((part.reshape((nctx,) + part.shape[2:]) for part in grouped[0]))
    dq_a = jnp.sum(grouped[1], axis=0)
    dq_b = jnp.sum(grouped[2], axis=0)
    pairs = pair_of_rank
    sliced = tuple(
        (lax.slice_in_dim(part, 0, 1 * lax.axis_size("ctx"), axis=0) for part in terms_all)
    )
    dk_a, dk_b, dv_a, dv_b = key_grads(sliced, query_a, query_b, dctx_a, dctx_b, pairs <= mine)
    dkey = jnp.concatenate([dk_a, dk_b], axis=2).reshape(
        1 * lax.axis_size("ctx"), seqs, width2, dmodel
    )
    dval = jnp.concatenate([dv_a, dv_b], axis=2).reshape(
        1 * lax.axis_size("ctx"), seqs, width2, dmodel
    )
    kv_grad = lax.psum_scatter(
        jnp.concatenate([dkey, dval], axis=-1), "ctx", scatter_dimension=0, tiled=True
    )
    dkey = kv_grad[0, :, :, :dmodel].reshape(seqs, width2, heads, HD)
    dval = kv_grad[0, :, :, dmodel:].reshape(seqs, width2, heads, HD)
    zero_half = jnp.zeros((seqs, blk, heads, HD), f32)
    dquery = jnp.concatenate([dq_a, dq_b + own_dq], axis=1)
    dkey = dkey + jnp.concatenate([zero_half, own_keys[1][0]], axis=1)
    dval = dval + jnp.concatenate([zero_half, own_keys[3][0]], axis=1)
    dqkv = jnp.concatenate(
        [
            rotate(dquery, places, -1.0).reshape(rows, dmodel),
            rotate(dkey, places, -1.0).reshape(rows, dmodel),
            dval.reshape(rows, dmodel),
        ],
        axis=1,
    )
    dqkv_b = dqkv.astype(bf)
    dnorm1 = rdot(dqkv_b, again[4])
    grad_x = (
        (
            grad_f
            + layer_norm_backward(dnorm1, hat1, rstd1, again[0])
            + layer_norm_backward(dnorm2, hat2, rstd2, again[2])
        )
        .astype(bf)
        .reshape(layer_in.shape)
    )
    vectors = (
        lax.psum_scatter(
            jnp.sum(dnorm1 * hat1, axis=0), ("fsdp", "ctx"), scatter_dimension=0, tiled=True
        ),
        lax.psum_scatter(jnp.sum(dnorm1, axis=0), ("fsdp", "ctx"), scatter_dimension=0, tiled=True),
        lax.psum_scatter(
            jnp.sum(dnorm2 * hat2, axis=0), ("fsdp", "ctx"), scatter_dimension=0, tiled=True
        ),
        lax.psum_scatter(jnp.sum(dnorm2, axis=0), ("fsdp", "ctx"), scatter_dimension=0, tiled=True),
        lax.psum_scatter(jnp.sum(dqkv, axis=0), ("fsdp", "ctx"), scatter_dimension=0, tiled=True),
        lax.psum_scatter(jnp.sum(grad_f, axis=0), ("fsdp", "ctx"), scatter_dimension=0, tiled=True),
        lax.psum_scatter(jnp.sum(dpre, axis=0), ("fsdp", "ctx"), scatter_dimension=0, tiled=True),
    )
    weights = (
        lax.psum_scatter(tdot(norm1, dqkv_b), ("fsdp", "ctx"), scatter_dimension=0, tiled=True),
        lax.psum_scatter(tdot(context, grad_b), ("fsdp", "ctx"), scatter_dimension=0, tiled=True),
        lax.psum_scatter(tdot(norm2, dpre_b), ("fsdp", "ctx"), scatter_dimension=0, tiled=True),
        lax.psum_scatter(tdot(grad_b, hidden), ("fsdp", "ctx"), scatter_dimension=0, tiled=True),
    )
    return (
        layer_out,
        grad_x,
        vectors[0],
        vectors[1],
        vectors[2],
        vectors[3],
        weights[0],
        vectors[4],
        weights[1],
        vectors[5],
        weights[2],
        vectors[6],
        weights[3],
        vectors[5],
    )


def span(lead, cols):
    return jnp.arange(lead, dtype=jnp.int32)[:, None] if cols else jnp.arange(lead, dtype=jnp.int32)


def turn(field, cosine, sine_low, sine_high):
    half = ROT // 2
    down = jnp.concatenate([field[:, half:], field[:, :half]], axis=1)
    up = jnp.concatenate([field[:, -half:], field[:, :-half]], axis=1)
    return field * cosine + down * sine_low + up * sine_high


def turn_tables(places, width):
    half = ROT // 2
    lane = jnp.arange(width, dtype=jnp.int32) % HD
    freqs = jnp.exp((lane % half).astype(jnp.float32) * (-2.0 * math.log(10000.0) / ROT))
    angle = places.astype(jnp.float32)[:, None] * freqs[None, :]
    cosine = jnp.where(lane < ROT, jnp.cos(angle), 1.0)
    sine = jnp.sin(angle)
    sine_low = jnp.where(lane < half, -sine, 0.0)
    sine_high = jnp.where((lane >= half) & (lane < ROT), sine, 0.0)
    return cosine, sine_low, sine_high


def headed(field, count):
    return field.reshape(field.shape[0], count, HD).transpose(1, 0, 2)


def joined(field):
    return field.transpose(1, 0, 2).reshape(field.shape[1], -1)


def bdot(form, left, right):
    return jnp.einsum(form, left, right, preferred_element_type=jnp.float32)


def head_shards(
    layer_in,
    grad_out,
    pair_of_rank,
    ln1_gain,
    ln1_bias,
    ln2_gain,
    ln2_bias,
    w_qkv,
    b_qkv,
    w_out,
    b_out,
    w_up,
    b_up,
    w_down,
    b_down,
):
    f32 = jnp.float32
    bf = jnp.bfloat16
    both = ("fsdp", "ctx")
    nctx = lax.axis_size("ctx")
    nf = lax.axis_size("fsdp")
    ndev = nctx * nf
    c = lax.axis_index("ctx")
    seqs, width2, dmodel = layer_in.shape[1:]
    blk = width2 // 2
    own_rows = seqs * width2
    ff = w_up.shape[1]
    hloc = dmodel // HD // nctx
    qw = hloc * HD
    fw = ff // nctx
    piece = dmodel // ndev
    scale = 1.0 / math.sqrt(HD)

    x_all = lax.all_gather(layer_in.reshape(own_rows, dmodel), "ctx", axis=0, tiled=True)
    vec = jnp.concatenate([ln1_gain, ln1_bias, ln2_gain, ln2_bias, b_out, b_down, b_qkv, b_up])
    vec = lax.all_gather(vec[None], both, axis=0, tiled=True)
    cuts = [piece] * 6 + [b_qkv.shape[0], b_up.shape[0]]
    fulls = []
    at = 0
    for cut in cuts:
        fulls.append(vec[:, at : at + cut].reshape(-1).astype(f32))
        at += cut
    gain1, bias1, gain2, bias2, bo, bd, bq, bu = fulls
    bq_c = lax.dynamic_slice_in_dim(bq.reshape(3, nctx, qw), c, 1, axis=1).reshape(1, 3 * qw)
    bu_c = lax.dynamic_slice_in_dim(bu, c * fw, fw).reshape(1, fw)

    def columns(parts):
        packed = jnp.concatenate([p.reshape(piece, nctx, -1) for p in parts], axis=-1)
        packed = packed.transpose(1, 0, 2)
        got = lax.all_to_all(packed, "ctx", split_axis=0, concat_axis=0, tiled=True)
        return got.reshape(nctx * piece, -1)

    wq = w_qkv.reshape(piece, 3, nctx, qw).transpose(0, 2, 1, 3)
    cols = lax.all_gather(columns([wq, w_up, w_down]), "fsdp", axis=0, tiled=True)
    wq_c = cols[:, : 3 * qw]
    wu_c = cols[:, 3 * qw : 3 * qw + fw]
    wd_c = cols[:, 3 * qw + fw :]
    there = [((nf * cc + f) , f * nctx + cc) for f in range(nf) for cc in range(nctx)]
    back = [(b, a) for a, b in there]
    wo_c = lax.all_gather(lax.ppermute(w_out, both, there), "fsdp", axis=0, tiled=True)
    g_own = grad_out.reshape(own_rows, dmodel)
    g_all = lax.all_gather(g_own, "ctx", axis=0, tiled=True)

    rows = x_all.shape[0]
    offsets = jnp.arange(blk, dtype=jnp.int32)
    slot_a = pair_of_rank[:, None] * blk + offsets[None, :]
    slot_b = (2 * nctx - 1 - pair_of_rank)[:, None] * blk + offsets[None, :]
    slots = jnp.concatenate([slot_a, slot_b], axis=1)[:, None, :]
    places = jnp.broadcast_to(slots, (nctx, seqs, width2)).reshape(rows)
    group = jnp.broadcast_to(span(seqs, False)[None, :, None], (nctx, seqs, width2)).reshape(rows)

    def hat_of(xf):
        row_mean = jnp.mean(xf, axis=-1, keepdims=True)
        centred = xf - row_mean
        rstd = lax.rsqrt(jnp.mean(centred * centred, axis=-1, keepdims=True) + EPS)
        return centred * rstd, rstd

    hat, _ = hat_of(x_all.astype(f32))
    norm1 = (hat * gain1 + bias1).astype(bf)
    norm2 = (hat * gain2 + bias2).astype(bf)
    qkv = jnp.dot(norm1, wq_c, preferred_element_type=f32) + bq_c
    cosine, sine_low, sine_high = turn_tables(places, qw)
    query = headed(turn(qkv[:, :qw], cosine, sine_low, sine_high).astype(bf), hloc)
    key = headed(turn(qkv[:, qw : 2 * qw], cosine, sine_low, sine_high).astype(bf), hloc)
    value = headed(qkv[:, 2 * qw :].astype(bf), hloc)
    visible = places[None, :] <= places[:, None]
    if seqs > 1:
        visible = visible & (group[None, :] == group[:, None])
    score = jnp.where(visible[None], bdot("hqd,hkd->hqk", query, key) * scale, NEG)
    top = jnp.max(score, axis=-1, keepdims=True)
    weight = jnp.exp(score - top)
    total = jnp.sum(weight, axis=-1, keepdims=True)
    mixed = bdot("hqk,hkd->hqd", weight.astype(bf), value)
    context = (mixed / total).astype(bf)
    lse = top + jnp.log(total)
    ctx_c = joined(context)

    pre = jnp.dot(norm2, wu_c, preferred_element_type=f32) + bu_c
    hidden = gelu_value(pre).astype(bf)
    part = rdot(hidden, wd_c) + jnp.dot(ctx_c, wo_c, preferred_element_type=f32)
    fwd = lax.psum_scatter(part.astype(bf), "ctx", scatter_dimension=0, tiled=True)
    x_own = layer_in.reshape(own_rows, dmodel).astype(f32)
    layer_out = (x_own + fwd.astype(f32) + (bo + bd)).astype(bf).reshape(layer_in.shape)

    dhidden = jnp.dot(g_all, wd_c, preferred_element_type=f32)
    dpre = dhidden * gelu_slope(pre)
    dpre_b = dpre.astype(bf)
    dnorm2 = rdot(dpre_b, wu_c)
    dctx = headed(rdot(g_all, wo_c).astype(bf), hloc)
    delta = jnp.sum(dctx.astype(f32) * context.astype(f32), axis=-1, keepdims=True)
    prob = jnp.exp(score - lse)
    dprob = bdot("hqd,hkd->hqk", dctx, value)
    ds = (scale * prob * (dprob - delta)).astype(bf)
    dquery = joined(bdot("hqk,hkd->hqd", ds, key))
    dkey = joined(bdot("hqk,hqd->hkd", ds, query))
    dvalue = joined(bdot("hqk,hqd->hkd", prob.astype(bf), dctx))
    dqkv = jnp.concatenate(
        [
            turn(dquery, cosine, -sine_low, -sine_high),
            turn(dkey, cosine, -sine_low, -sine_high),
            dvalue,
        ],
        axis=1,
    )
    dqkv_b = dqkv.astype(bf)
    dnorm1 = rdot(dqkv_b, wq_c)
    gsum = (dnorm1 * gain1 + dnorm2 * gain2).astype(bf)
    gsum = lax.psum_scatter(gsum, "ctx", scatter_dimension=0, tiled=True).astype(f32)
    hat_own, rstd_own = hat_of(x_own)
    g_ownf = g_own.astype(f32)
    grad_x = (
        g_ownf
        + rstd_own
        * (
            gsum
            - jnp.mean(gsum, axis=-1, keepdims=True)
            - hat_own * jnp.mean(gsum * hat_own, axis=-1, keepdims=True)
        )
    ).astype(bf).reshape(layer_in.shape)

    wide = jnp.concatenate([tdot(norm1, dqkv_b), tdot(norm2, dpre_b), tdot(g_all, hidden)], axis=1)
    wide = lax.psum_scatter(wide.astype(bf), "fsdp", scatter_dimension=0, tiled=True)
    wide = lax.all_to_all(
        wide.reshape(nctx, piece, -1), "ctx", split_axis=0, concat_axis=0, tiled=True
    )
    wide = wide.transpose(1, 0, 2).astype(f32)
    grad_qkv = (
        wide[:, :, : 3 * qw].reshape(piece, nctx, 3, qw).transpose(0, 2, 1, 3).reshape(piece, -1)
    )
    grad_up = wide[:, :, 3 * qw : 3 * qw + fw].reshape(piece, ff)
    grad_down = wide[:, :, 3 * qw + fw :].reshape(piece, ff)
    rows_out = tdot(ctx_c, g_all)
    rows_out = lax.psum_scatter(rows_out.astype(bf), "fsdp", scatter_dimension=0, tiled=True)
    grad_wout = lax.ppermute(rows_out, both, back).astype(f32)

    sum_q = jnp.zeros((3, nctx, qw), f32)
    sum_q = lax.dynamic_update_slice_in_dim(
        sum_q, jnp.sum(dqkv, axis=0).reshape(3, 1, qw), c, axis=1
    ).reshape(ndev, -1)
    sum_u = lax.dynamic_update_slice_in_dim(
        jnp.zeros((ff,), f32), jnp.sum(dpre, axis=0), c * fw, axis=0
    ).reshape(ndev, -1)
    sums = [
        jnp.sum(dnorm1 * hat, axis=0).reshape(ndev, -1),
        jnp.sum(dnorm1, axis=0).reshape(ndev, -1),
        jnp.sum(dnorm2 * hat, axis=0).reshape(ndev, -1),
        jnp.sum(dnorm2, axis=0).reshape(ndev, -1),
        jnp.sum(g_ownf, axis=0).reshape(ndev, -1),
        sum_q,
        sum_u,
    ]
    sums = lax.psum_scatter(
        jnp.concatenate(sums, axis=1), both, scatter_dimension=0, tiled=True
    ).reshape(-1)
    ends = [piece * i for i in range(6)] + [5 * piece + b_qkv.shape[0], sums.shape[0]]
    vs = [sums[a:b] for a, b in zip(ends[:-1], ends[1:])]
    return (
        layer_out,
        grad_x,
        vs[0],
        vs[1],
        vs[2],
        vs[3],
        grad_qkv,
        vs[5],
        grad_wout,
        vs[4],
        grad_up,
        vs[6],
        grad_down,
        vs[4],
    )


def solution(mesh):
    nctx = mesh.shape["ctx"]

    def pick(layer_in, *rest):
        heads = layer_in.shape[-1] // HD
        whole = heads % nctx == 0
        return (head_shards if whole else shards)(layer_in, *rest)

    return jax.shard_map(
        pick,
        mesh=mesh,
        in_specs=(
            P("ctx", "fsdp", None, None),
            P("ctx", "fsdp", None, None),
            P(),
            P(("fsdp", "ctx")),
            P(("fsdp", "ctx")),
            P(("fsdp", "ctx")),
            P(("fsdp", "ctx")),
            P(("fsdp", "ctx"), None),
            P(("fsdp", "ctx")),
            P(("fsdp", "ctx"), None),
            P(("fsdp", "ctx")),
            P(("fsdp", "ctx"), None),
            P(("fsdp", "ctx")),
            P(("fsdp", "ctx"), None),
            P(("fsdp", "ctx")),
        ),
        out_specs=(
            P("ctx", "fsdp", None, None),
            P("ctx", "fsdp", None, None),
            P(("fsdp", "ctx")),
            P(("fsdp", "ctx")),
            P(("fsdp", "ctx")),
            P(("fsdp", "ctx")),
            P(("fsdp", "ctx"), None),
            P(("fsdp", "ctx")),
            P(("fsdp", "ctx"), None),
            P(("fsdp", "ctx")),
            P(("fsdp", "ctx"), None),
            P(("fsdp", "ctx")),
            P(("fsdp", "ctx"), None),
            P(("fsdp", "ctx")),
        ),
        check_vma=False,
    )
```

```python
import math

import jax
import jax.numpy as jnp
from jax import lax
from jax.sharding import PartitionSpec as P

HD = 64
ROT = 16
LANES = 128


EPS = 1e-05
NEG = -1e30
ROOT_HALF = 0.7071067811865476
INV_ROOT_TAU = 0.3989422804014327


def norm_parts(xf, scale_weight, shift_bias):
    row_mean = jnp.mean(xf, axis=-1, keepdims=True)
    centred_input = xf - row_mean
    inverse_deviation = lax.rsqrt(
        jnp.mean(centred_input * centred_input, axis=-1, keepdims=True) + EPS
    )
    normalized_input = centred_input * inverse_deviation
    return (
        normalized_input * scale_weight.astype(jnp.float32) + shift_bias.astype(jnp.float32),
        normalized_input,
        inverse_deviation,
    )


def layer_norm_backward(norm_output_gradient, normalized_input, inverse_deviation, scale_weight):
    normalized_gradient = norm_output_gradient * scale_weight.astype(jnp.float32)
    return inverse_deviation * (
        normalized_gradient
        - jnp.mean(normalized_gradient, axis=-1, keepdims=True)
        - normalized_input
        * jnp.mean(normalized_gradient * normalized_input, axis=-1, keepdims=True)
    )


def gelu_value(u):
    return 0.5 * u * (1.0 + lax.erf(u * ROOT_HALF))


def gelu_slope(u):
    return 0.5 * (1.0 + lax.erf(u * ROOT_HALF)) + u * jnp.exp(-0.5 * u * u) * INV_ROOT_TAU


def rotate(field, place, sign):
    half = ROT // 2
    freqs = jnp.exp(jnp.arange(half).astype(jnp.float32) * (-2.0 * math.log(10000.0) / ROT))
    angle = place.astype(jnp.float32)[..., None] * freqs
    cosine = jnp.cos(angle)[..., None, :]
    sine = sign * jnp.sin(angle)[..., None, :]
    first = field[..., :half]
    second = field[..., half:ROT]
    return jnp.concatenate(
        [first * cosine - second * sine, second * cosine + first * sine, field[..., rot_end() :]],
        axis=-1,
    )


def rot_end():
    return ROT


def leading(field, letters):
    return "n" + letters if field.ndim == 5 else letters


def product(left, left_letters, right, right_letters, result):
    form = leading(left, left_letters) + "," + leading(right, right_letters) + "->" + result
    return jnp.einsum(form, left, right, preferred_element_type=jnp.float32)


def selectors(sel):
    return (sel[:, None, None, None, None], sel[:, None, None, None], sel[:, None])


def visibility(sel, qpa, qpb, kpa, kpb):
    chosen = sel[:, None]
    key_place = jnp.where(chosen, kpa, kpb)
    query_place = jnp.where(chosen, qpa, qpb)
    return (key_place[:, None, :] <= query_place[:, :, None])[:, None, None]


def online_update(state, qa, qb, ka, kb, va, vb, qpa, qpb, kpa, kpb, sel, with_first, scale):
    top_a, total_a, acc_a, top_b, total_b, acc_b = state
    sel5, sel4, sel2 = selectors(sel)
    query_two = jnp.where(sel5, qa, qb)
    key_two = jnp.where(sel5, ka, kb)
    value_two = jnp.where(sel5, va, vb)
    visible = visibility(sel, qpa, qpb, kpa, kpb)
    score = jnp.where(visible, product(query_two, "sqhd", key_two, "skhd", "nshqk") * scale, NEG)
    peak_a = jnp.max(jnp.where(sel5, score, NEG), axis=(0, 4))
    peak_b = jnp.max(jnp.where(sel5, NEG, score), axis=(0, 4))
    if with_first:
        score_one = product(qb, "sqhd", ka, "skhd", "nshqk") * scale
        peak_b = jnp.maximum(peak_b, jnp.max(score_one, axis=(0, 4)))
    new_a = jnp.maximum(top_a, peak_a)
    new_b = jnp.maximum(top_b, peak_b)
    lifted = jnp.where(sel5, new_a[..., None], new_b[..., None])
    weight = jnp.where(visible, jnp.exp(score - lifted), 0.0)
    mixed = product(weight.astype(jnp.bfloat16), "shqk", value_two, "skhd", "nshqd")
    mass = jnp.sum(weight, axis=4)
    add_total_a = jnp.sum(jnp.where(sel4, mass, 0.0), axis=0)
    add_total_b = jnp.sum(jnp.where(sel4, 0.0, mass), axis=0)
    add_acc_a = jnp.sum(jnp.where(sel5, mixed, 0.0), axis=0)
    add_acc_b = jnp.sum(jnp.where(sel5, 0.0, mixed), axis=0)
    if with_first:
        weight_one = jnp.exp(score_one - new_b[..., None])
        add_total_b = add_total_b + jnp.sum(weight_one, axis=(0, 4))
        add_acc_b = add_acc_b + product(weight_one.astype(jnp.bfloat16), "shqk", va, "skhd", "shqd")
    decay_a = jnp.exp(top_a - new_a)
    decay_b = jnp.exp(top_b - new_b)
    return (
        new_a,
        total_a * decay_a + add_total_a,
        acc_a * decay_a[..., None] + add_acc_a,
        new_b,
        total_b * decay_b + add_total_b,
        acc_b * decay_b[..., None] + add_acc_b,
    )


def pair_terms(
    qa,
    qb,
    ka,
    kb,
    va,
    vb,
    da,
    db,
    lsea,
    lseb,
    dela,
    delb,
    qpa,
    qpb,
    kpa,
    kpb,
    sel,
    with_first,
    scale,
):
    sel5, sel4, sel2 = selectors(sel)
    query_two = jnp.where(sel5, qa, qb)
    key_two = jnp.where(sel5, ka, kb)
    value_two = jnp.where(sel5, va, vb)
    dctx_two = jnp.where(sel5, da, db)
    lse_two = jnp.where(sel4, lsea, lseb)
    delta_two = jnp.where(sel4, dela, delb)
    visible = visibility(sel, qpa, qpb, kpa, kpb)
    score = jnp.where(visible, product(query_two, "sqhd", key_two, "skhd", "nshqk") * scale, NEG)
    prob = jnp.exp(score - lse_two[..., None])
    dprob = product(dctx_two, "sqhd", value_two, "skhd", "nshqk")
    dscore = (scale * prob * (dprob - delta_two[..., None])).astype(jnp.bfloat16)
    first_ds = None
    first_prob = None
    if with_first:
        score_one = product(qb, "sqhd", ka, "skhd", "nshqk") * scale
        prob_one = jnp.exp(score_one - lseb[..., None])
        dprob_one = product(db, "sqhd", va, "skhd", "nshqk")
        first_ds = (scale * prob_one * (dprob_one - delb[..., None])).astype(jnp.bfloat16)
        first_prob = prob_one.astype(jnp.bfloat16)
    return (first_ds, first_prob, dscore, prob.astype(jnp.bfloat16))


def query_grads(terms, ka, kb, sel):
    sel5, sel4, sel2 = selectors(sel)
    key_two = jnp.where(sel5, ka, kb)
    dq_two = product(terms[2], "shqk", key_two, "skhd", "nsqhd")
    dq_a = jnp.where(sel5, dq_two, 0.0)
    dq_b = jnp.where(sel5, 0.0, dq_two)
    if terms[0] is not None:
        dq_b = dq_b + product(terms[0], "shqk", ka, "skhd", "nsqhd")
    return (dq_a, dq_b)


def key_grads(terms, qa, qb, da, db, sel):
    sel5, sel4, sel2 = selectors(sel)
    query_two = jnp.where(sel5, qa, qb)
    dctx_two = jnp.where(sel5, da, db)
    dk_two = product(terms[2], "shqk", query_two, "sqhd", "nskhd")
    dv_two = product(terms[3], "shqk", dctx_two, "sqhd", "nskhd")
    dk_a = jnp.where(sel5, dk_two, 0.0)
    dk_b = jnp.where(sel5, 0.0, dk_two)
    dv_a = jnp.where(sel5, dv_two, 0.0)
    dv_b = jnp.where(sel5, 0.0, dv_two)
    if terms[0] is not None:
        dk_a = dk_a + product(terms[0], "shqk", qb, "sqhd", "nskhd")
        dv_a = dv_a + product(terms[1], "shqk", db, "sqhd", "nskhd")
    return (dk_a, dk_b, dv_a, dv_b)


def tdot(left, right):
    return lax.dot_general(
        left, right, (((0,), (0,)), ((), ())), preferred_element_type=jnp.float32
    )


def rdot(left, right):
    return lax.dot_general(
        left, right, (((1,), (1,)), ((), ())), preferred_element_type=jnp.float32
    )


def shards(
    layer_in,
    grad_out,
    pair_of_rank,
    ln1_gain,
    ln1_bias,
    ln2_gain,
    ln2_bias,
    w_qkv,
    b_qkv,
    w_out,
    b_out,
    w_up,
    b_up,
    w_down,
    b_down,
):
    f32 = jnp.float32
    bf = jnp.bfloat16
    nctx = lax.axis_size("ctx")
    mine = pair_of_rank[lax.axis_index("ctx")]
    seqs = layer_in.shape[1]
    width2 = layer_in.shape[2]
    dmodel = layer_in.shape[3]
    blk = width2 // 2
    rows = seqs * width2
    heads = dmodel // HD
    scale = 1.0 / math.sqrt(HD)
    offsets = jnp.arange(blk, dtype=jnp.int32)
    place_a = mine * blk + offsets
    place_b = (2 * nctx - 1 - mine) * blk + offsets
    places = jnp.concatenate([place_a, place_b])
    params = (
        ln1_gain,
        ln1_bias,
        ln2_gain,
        ln2_bias,
        w_qkv,
        b_qkv,
        w_out,
        b_out,
        w_up,
        b_up,
        w_down,
        b_down,
    )
    full = (
        lax.all_gather(params[0], ("fsdp", "ctx"), axis=0, tiled=True),
        lax.all_gather(params[1], ("fsdp", "ctx"), axis=0, tiled=True),
        lax.all_gather(params[2], ("fsdp", "ctx"), axis=0, tiled=True),
        lax.all_gather(params[3], ("fsdp", "ctx"), axis=0, tiled=True),
        lax.all_gather(params[4], ("fsdp", "ctx"), axis=0, tiled=True),
        lax.all_gather(params[5], ("fsdp", "ctx"), axis=0, tiled=True),
        lax.all_gather(params[6], ("fsdp", "ctx"), axis=0, tiled=True),
        lax.all_gather(params[7], ("fsdp", "ctx"), axis=0, tiled=True),
        lax.all_gather(params[8], ("fsdp", "ctx"), axis=0, tiled=True),
        lax.all_gather(params[9], ("fsdp", "ctx"), axis=0, tiled=True),
        lax.all_gather(params[10], ("fsdp", "ctx"), axis=0, tiled=True),
        lax.all_gather(params[11], ("fsdp", "ctx"), axis=0, tiled=True),
    )
    xf = layer_in.reshape(rows, dmodel).astype(f32)
    norm1, hat1, rstd1 = norm_parts(xf, full[0], full[1])
    norm2, hat2, rstd2 = norm_parts(xf, full[2], full[3])
    norm1 = norm1.astype(bf)
    norm2 = norm2.astype(bf)
    qkv = jnp.dot(norm1, full[4], preferred_element_type=f32) + full[5].astype(f32)
    query = rotate(qkv[:, :dmodel].reshape(seqs, width2, heads, HD), places, 1.0).astype(bf)
    key = rotate(qkv[:, dmodel : 2 * dmodel].reshape(seqs, width2, heads, HD), places, 1.0).astype(
        bf
    )
    value = qkv[:, 2 * dmodel :].reshape(seqs, width2, heads, HD).astype(bf)
    query_a = query[:, :blk]
    query_b = query[:, blk:]
    key_b = key[:, blk:]
    value_b = value[:, blk:]
    lone = jnp.zeros((1,), dtype=bool)
    empty_top = jnp.full((seqs, heads, blk), NEG, f32)
    empty_total = jnp.zeros((seqs, heads, blk), f32)
    empty_acc = jnp.zeros((seqs, heads, blk, HD), f32)
    state = (empty_top, empty_total, empty_acc, empty_top, empty_total, empty_acc)
    state = online_update(
        state,
        query_a,
        query_b,
        key_b[None],
        key_b[None],
        value_b[None],
        value_b[None],
        place_a,
        place_b,
        place_b[None],
        place_b[None],
        lone,
        False,
        scale,
    )

    def key_parts(kpiece, vpiece, first):
        count = kpiece.shape[0]
        pairs = lax.dynamic_slice_in_dim(pair_of_rank, first, count)
        keys = kpiece.reshape(count, seqs, width2, heads, HD)
        values = vpiece.reshape(count, seqs, width2, heads, HD)
        kplace_a = pairs[:, None] * blk + offsets[None, :]
        kplace_b = (2 * nctx - 1 - pairs)[:, None] * blk + offsets[None, :]
        return (
            keys[:, :, :blk],
            keys[:, :, blk:],
            values[:, :, :blk],
            values[:, :, blk:],
            kplace_a,
            kplace_b,
            pairs,
        )

    key_send = key.reshape(1, seqs, width2, dmodel)
    value_send = value.reshape(1, seqs, width2, dmodel)
    ka, kb, va, vb, kpa, kpb, pairs = key_parts(
        lax.all_gather(key_send, "ctx", axis=0, tiled=True),
        lax.all_gather(value_send, "ctx", axis=0, tiled=True),
        jnp.int32(0),
    )
    state = online_update(
        state,
        query_a,
        query_b,
        ka,
        kb,
        va,
        vb,
        place_a,
        place_b,
        kpa,
        kpb,
        pairs <= mine,
        True,
        scale,
    )
    top_a, total_a, acc_a, top_b, total_b, acc_b = state
    context4 = jnp.concatenate([acc_a / total_a[..., None], acc_b / total_b[..., None]], axis=2)
    lse = jnp.concatenate([top_a + jnp.log(total_a), top_b + jnp.log(total_b)], axis=2)
    context = context4.transpose(0, 2, 1, 3).reshape(rows, dmodel).astype(bf)
    attn = jnp.dot(context, full[6], preferred_element_type=f32) + full[7].astype(f32)
    pre = jnp.dot(norm2, full[8], preferred_element_type=f32) + full[9].astype(f32)
    hidden = gelu_value(pre).astype(bf)
    mlp = rdot(hidden, full[10]) + full[11].astype(f32)
    layer_out = (xf + attn + mlp).astype(bf).reshape(layer_in.shape)
    again = (
        lax.all_gather(params[0], ("fsdp", "ctx"), axis=0, tiled=True),
        lax.all_gather(params[1], ("fsdp", "ctx"), axis=0, tiled=True),
        lax.all_gather(params[2], ("fsdp", "ctx"), axis=0, tiled=True),
        lax.all_gather(params[3], ("fsdp", "ctx"), axis=0, tiled=True),
        lax.all_gather(params[4], ("fsdp", "ctx"), axis=0, tiled=True),
        lax.all_gather(params[5], ("fsdp", "ctx"), axis=0, tiled=True),
        lax.all_gather(params[6], ("fsdp", "ctx"), axis=0, tiled=True),
        lax.all_gather(params[7], ("fsdp", "ctx"), axis=0, tiled=True),
        lax.all_gather(params[8], ("fsdp", "ctx"), axis=0, tiled=True),
        lax.all_gather(params[9], ("fsdp", "ctx"), axis=0, tiled=True),
        lax.all_gather(params[10], ("fsdp", "ctx"), axis=0, tiled=True),
        lax.all_gather(params[11], ("fsdp", "ctx"), axis=0, tiled=True),
    )
    grad_b = grad_out.reshape(rows, dmodel)
    grad_f = grad_b.astype(f32)
    dhidden = jnp.dot(grad_b, again[10], preferred_element_type=f32)
    dpre = dhidden * gelu_slope(pre)
    dpre_b = dpre.astype(bf)
    dnorm2 = rdot(dpre_b, again[8])
    dcontext = rdot(grad_b, again[6]).astype(bf)
    dctx4 = dcontext.reshape(seqs, width2, heads, HD)
    delta = jnp.sum(
        dctx4.astype(f32) * context.reshape(seqs, width2, heads, HD).astype(f32), axis=-1
    ).transpose(0, 2, 1)
    dctx_a = dctx4[:, :blk]
    dctx_b = dctx4[:, blk:]
    lse_a = lse[..., :blk]
    lse_b = lse[..., blk:]
    delta_a = delta[..., :blk]
    delta_b = delta[..., blk:]
    own = pair_terms(
        query_b,
        query_b,
        key_b[None],
        key_b[None],
        value_b[None],
        value_b[None],
        dctx_b,
        dctx_b,
        lse_b,
        lse_b,
        delta_b,
        delta_b,
        place_b,
        place_b,
        place_b[None],
        place_b[None],
        lone,
        False,
        scale,
    )
    own_dq = query_grads(own, key_b[None], key_b[None], lone)[1][0]
    own_keys = key_grads(own, query_b, query_b, dctx_b, dctx_b, lone)
    gathered = (
        lax.all_gather(key_send, "ctx", axis=0, tiled=True),
        lax.all_gather(value_send, "ctx", axis=0, tiled=True),
    )
    groups = math.gcd(nctx, 8)
    per = nctx // groups

    def group_terms(args):
        kpiece, vpiece, first = args
        ka, kb, va, vb, kpa, kpb, pairs = key_parts(kpiece, vpiece, first)
        sel = pairs <= mine
        terms = pair_terms(
            query_a,
            query_b,
            ka,
            kb,
            va,
            vb,
            dctx_a,
            dctx_b,
            lse_a,
            lse_b,
            delta_a,
            delta_b,
            place_a,
            place_b,
            kpa,
            kpb,
            sel,
            True,
            scale,
        )
        dq_a, dq_b = query_grads(terms, ka, kb, sel)
        return (terms, jnp.sum(dq_a, axis=0), jnp.sum(dq_b, axis=0))

    grouped = lax.map(
        group_terms,
        (
            gathered[0].reshape(groups, per, seqs, width2, dmodel),
            gathered[1].reshape(groups, per, seqs, width2, dmodel),
            jnp.arange(groups, dtype=jnp.int32) * per,
        ),
    )
    terms_all = tuple((part.reshape((nctx,) + part.shape[2:]) for part in grouped[0]))
    dq_a = jnp.sum(grouped[1], axis=0)
    dq_b = jnp.sum(grouped[2], axis=0)
    pairs = pair_of_rank
    sliced = tuple(
        (lax.slice_in_dim(part, 0, 1 * lax.axis_size("ctx"), axis=0) for part in terms_all)
    )
    dk_a, dk_b, dv_a, dv_b = key_grads(sliced, query_a, query_b, dctx_a, dctx_b, pairs <= mine)
    dkey = jnp.concatenate([dk_a, dk_b], axis=2).reshape(
        1 * lax.axis_size("ctx"), seqs, width2, dmodel
    )
    dval = jnp.concatenate([dv_a, dv_b], axis=2).reshape(
        1 * lax.axis_size("ctx"), seqs, width2, dmodel
    )
    kv_grad = lax.psum_scatter(
        jnp.concatenate([dkey, dval], axis=-1), "ctx", scatter_dimension=0, tiled=True
    )
    dkey = kv_grad[0, :, :, :dmodel].reshape(seqs, width2, heads, HD)
    dval = kv_grad[0, :, :, dmodel:].reshape(seqs, width2, heads, HD)
    zero_half = jnp.zeros((seqs, blk, heads, HD), f32)
    dquery = jnp.concatenate([dq_a, dq_b + own_dq], axis=1)
    dkey = dkey + jnp.concatenate([zero_half, own_keys[1][0]], axis=1)
    dval = dval + jnp.concatenate([zero_half, own_keys[3][0]], axis=1)
    dqkv = jnp.concatenate(
        [
            rotate(dquery, places, -1.0).reshape(rows, dmodel),
            rotate(dkey, places, -1.0).reshape(rows, dmodel),
            dval.reshape(rows, dmodel),
        ],
        axis=1,
    )
    dqkv_b = dqkv.astype(bf)
    dnorm1 = rdot(dqkv_b, again[4])
    grad_x = (
        (
            grad_f
            + layer_norm_backward(dnorm1, hat1, rstd1, again[0])
            + layer_norm_backward(dnorm2, hat2, rstd2, again[2])
        )
        .astype(bf)
        .reshape(layer_in.shape)
    )
    vectors = (
        lax.psum_scatter(
            jnp.sum(dnorm1 * hat1, axis=0), ("fsdp", "ctx"), scatter_dimension=0, tiled=True
        ),
        lax.psum_scatter(jnp.sum(dnorm1, axis=0), ("fsdp", "ctx"), scatter_dimension=0, tiled=True),
        lax.psum_scatter(
            jnp.sum(dnorm2 * hat2, axis=0), ("fsdp", "ctx"), scatter_dimension=0, tiled=True
        ),
        lax.psum_scatter(jnp.sum(dnorm2, axis=0), ("fsdp", "ctx"), scatter_dimension=0, tiled=True),
        lax.psum_scatter(jnp.sum(dqkv, axis=0), ("fsdp", "ctx"), scatter_dimension=0, tiled=True),
        lax.psum_scatter(jnp.sum(grad_f, axis=0), ("fsdp", "ctx"), scatter_dimension=0, tiled=True),
        lax.psum_scatter(jnp.sum(dpre, axis=0), ("fsdp", "ctx"), scatter_dimension=0, tiled=True),
    )
    weights = (
        lax.psum_scatter(tdot(norm1, dqkv_b), ("fsdp", "ctx"), scatter_dimension=0, tiled=True),
        lax.psum_scatter(tdot(context, grad_b), ("fsdp", "ctx"), scatter_dimension=0, tiled=True),
        lax.psum_scatter(tdot(norm2, dpre_b), ("fsdp", "ctx"), scatter_dimension=0, tiled=True),
        lax.psum_scatter(tdot(grad_b, hidden), ("fsdp", "ctx"), scatter_dimension=0, tiled=True),
    )
    return (
        layer_out,
        grad_x,
        vectors[0],
        vectors[1],
        vectors[2],
        vectors[3],
        weights[0],
        vectors[4],
        weights[1],
        vectors[5],
        weights[2],
        vectors[6],
        weights[3],
        vectors[5],
    )


def span(lead, cols):
    return jnp.arange(lead, dtype=jnp.int32)[:, None] if cols else jnp.arange(lead, dtype=jnp.int32)


def turn(field, cosine, sine_low, sine_high):
    half = ROT // 2
    down = jnp.concatenate([field[:, half:], field[:, :half]], axis=1)
    up = jnp.concatenate([field[:, -half:], field[:, :-half]], axis=1)
    return field * cosine + down * sine_low + up * sine_high


def turn_tables(places, width):
    half = ROT // 2
    lane = jnp.arange(width, dtype=jnp.int32) % HD
    freqs = jnp.exp((lane % half).astype(jnp.float32) * (-2.0 * math.log(10000.0) / ROT))
    angle = places.astype(jnp.float32)[:, None] * freqs[None, :]
    cosine = jnp.where(lane < ROT, jnp.cos(angle), 1.0)
    sine = jnp.sin(angle)
    sine_low = jnp.where(lane < half, -sine, 0.0)
    sine_high = jnp.where((lane >= half) & (lane < ROT), sine, 0.0)
    return cosine, sine_low, sine_high


def headed(field, count):
    return field.reshape(field.shape[0], count, HD).transpose(1, 0, 2)


def joined(field):
    return field.transpose(1, 0, 2).reshape(field.shape[1], -1)


def bdot(form, left, right):
    return jnp.einsum(form, left, right, preferred_element_type=jnp.float32)


def head_shards(
    layer_in,
    grad_out,
    pair_of_rank,
    ln1_gain,
    ln1_bias,
    ln2_gain,
    ln2_bias,
    w_qkv,
    b_qkv,
    w_out,
    b_out,
    w_up,
    b_up,
    w_down,
    b_down,
):
    f32 = jnp.float32
    bf = jnp.bfloat16
    both = ("fsdp", "ctx")
    nctx = lax.axis_size("ctx")
    nf = lax.axis_size("fsdp")
    ndev = nctx * nf
    c = lax.axis_index("ctx")
    seqs, width2, dmodel = layer_in.shape[1:]
    blk = width2 // 2
    own_rows = seqs * width2
    ff = w_up.shape[1]
    hloc = dmodel // HD // nctx
    qw = hloc * HD
    fw = ff // nctx
    piece = dmodel // ndev
    scale = 1.0 / math.sqrt(HD)

    x_all = lax.all_gather(layer_in.reshape(own_rows, dmodel), "ctx", axis=0, tiled=True)
    def columns(parts):
        packed = jnp.concatenate([p.reshape(piece, nctx, -1) for p in parts], axis=-1)
        packed = packed.transpose(1, 0, 2)
        got = lax.all_to_all(packed, "ctx", split_axis=0, concat_axis=0, tiled=True)
        return got.reshape(nctx * piece, -1)

    wq = w_qkv.reshape(piece, 3, nctx, qw).transpose(0, 2, 1, 3)
    vec = jnp.concatenate([ln1_gain, ln1_bias, ln2_gain, ln2_bias, b_out, b_down, b_qkv, b_up])
    vw = LANES * -(-vec.shape[0] // (piece * LANES))
    vec_pad = jnp.pad(vec, (0, piece * vw - vec.shape[0])).reshape(piece, 1, vw)
    vec_pad = jnp.broadcast_to(vec_pad, (piece, nctx, vw))
    cols = lax.all_gather(columns([wq, w_up, w_down, vec_pad]), "fsdp", axis=0, tiled=True)
    g_own = grad_out.reshape(own_rows, dmodel)
    cols, g_send = lax.optimization_barrier((cols, g_own))
    got = cols[:, 3 * qw + 2 * fw :].reshape(ndev, piece * vw)
    cuts = [piece] * 6 + [b_qkv.shape[0], b_up.shape[0]]
    fulls = []
    at = 0
    for cut in cuts:
        fulls.append(got[:, at : at + cut].reshape(-1).astype(f32))
        at += cut
    gain1, bias1, gain2, bias2, bo, bd, bq, bu = fulls
    bq_c = lax.dynamic_slice_in_dim(bq.reshape(3, nctx, qw), c, 1, axis=1).reshape(1, 3 * qw)
    bu_c = lax.dynamic_slice_in_dim(bu, c * fw, fw).reshape(1, fw)
    wq_c = cols[:, : 3 * qw]
    wu_c = cols[:, 3 * qw : 3 * qw + fw]
    wd_c = cols[:, 3 * qw + fw : 3 * qw + 2 * fw]
    there = [((nf * cc + f) , f * nctx + cc) for f in range(nf) for cc in range(nctx)]
    back = [(b, a) for a, b in there]
    wo_c = lax.all_gather(lax.ppermute(w_out, both, there), "fsdp", axis=0, tiled=True)
    g_all = lax.all_gather(g_send, "ctx", axis=0, tiled=True)

    rows = x_all.shape[0]
    offsets = jnp.arange(blk, dtype=jnp.int32)
    slot_a = pair_of_rank[:, None] * blk + offsets[None, :]
    slot_b = (2 * nctx - 1 - pair_of_rank)[:, None] * blk + offsets[None, :]
    slots = jnp.concatenate([slot_a, slot_b], axis=1)[:, None, :]
    places = jnp.broadcast_to(slots, (nctx, seqs, width2)).reshape(rows)
    group = jnp.broadcast_to(span(seqs, False)[None, :, None], (nctx, seqs, width2)).reshape(rows)

    def hat_of(xf):
        row_mean = jnp.mean(xf, axis=-1, keepdims=True)
        centred = xf - row_mean
        rstd = lax.rsqrt(jnp.mean(centred * centred, axis=-1, keepdims=True) + EPS)
        return centred * rstd, rstd

    hat, _ = hat_of(x_all.astype(f32))
    norm1 = (hat * gain1 + bias1).astype(bf)
    norm2 = (hat * gain2 + bias2).astype(bf)
    qkv = jnp.dot(norm1, wq_c, preferred_element_type=f32) + bq_c
    cosine, sine_low, sine_high = turn_tables(places, qw)
    query = headed(turn(qkv[:, :qw], cosine, sine_low, sine_high).astype(bf), hloc)
    key = headed(turn(qkv[:, qw : 2 * qw], cosine, sine_low, sine_high).astype(bf), hloc)
    value = headed(qkv[:, 2 * qw :].astype(bf), hloc)
    visible = places[None, :] <= places[:, None]
    if seqs > 1:
        visible = visible & (group[None, :] == group[:, None])
    score = jnp.where(visible[None], bdot("hqd,hkd->hqk", query, key) * scale, NEG)
    top = jnp.max(score, axis=-1, keepdims=True)
    weight = jnp.exp(score - top)
    total = jnp.sum(weight, axis=-1, keepdims=True)
    mixed = bdot("hqk,hkd->hqd", weight.astype(bf), value)
    context = (mixed / total).astype(bf)
    lse = top + jnp.log(total)
    ctx_c = joined(context)

    pre = jnp.dot(norm2, wu_c, preferred_element_type=f32) + bu_c
    hidden = gelu_value(pre).astype(bf)
    part = rdot(hidden, wd_c) + jnp.dot(ctx_c, wo_c, preferred_element_type=f32)
    fwd = lax.all_to_all(
        part.astype(bf).reshape(nctx, own_rows, dmodel), "ctx", split_axis=0, concat_axis=0, tiled=True
    )
    fwd = jnp.sum(fwd.astype(f32), axis=0)
    x_own = layer_in.reshape(own_rows, dmodel).astype(f32)
    layer_out = (x_own + fwd + (bo + bd)).astype(bf).reshape(layer_in.shape)

    dhidden = jnp.dot(g_all, wd_c, preferred_element_type=f32)
    dpre = dhidden * gelu_slope(pre)
    dpre_b = dpre.astype(bf)
    dnorm2 = rdot(dpre_b, wu_c)
    dctx = headed(rdot(g_all, wo_c).astype(bf), hloc)
    delta = jnp.sum(dctx.astype(f32) * context.astype(f32), axis=-1, keepdims=True)
    prob = jnp.exp(score - lse)
    dprob = bdot("hqd,hkd->hqk", dctx, value)
    ds = (scale * prob * (dprob - delta)).astype(bf)
    dquery = joined(bdot("hqk,hkd->hqd", ds, key))
    dkey = joined(bdot("hqk,hqd->hkd", ds, query))
    dvalue = joined(bdot("hqk,hqd->hkd", prob.astype(bf), dctx))
    dqkv = jnp.concatenate(
        [
            turn(dquery, cosine, -sine_low, -sine_high),
            turn(dkey, cosine, -sine_low, -sine_high),
            dvalue,
        ],
        axis=1,
    )
    dqkv_b = dqkv.astype(bf)
    dnorm1 = rdot(dqkv_b, wq_c)
    gsum = (dnorm1 * gain1 + dnorm2 * gain2).astype(bf)
    gsum = lax.psum_scatter(gsum, "ctx", scatter_dimension=0, tiled=True).astype(f32)
    hat_own, rstd_own = hat_of(x_own)
    g_ownf = g_own.astype(f32)
    grad_x = (
        g_ownf
        + rstd_own
        * (
            gsum
            - jnp.mean(gsum, axis=-1, keepdims=True)
            - hat_own * jnp.mean(gsum * hat_own, axis=-1, keepdims=True)
        )
    ).astype(bf).reshape(layer_in.shape)

    sum_q = jnp.zeros((3, nctx, qw), f32)
    sum_q = lax.dynamic_update_slice_in_dim(
        sum_q, jnp.sum(dqkv, axis=0).reshape(3, 1, qw), c, axis=1
    ).reshape(ndev, -1)
    sum_u = lax.dynamic_update_slice_in_dim(
        jnp.zeros((ff,), f32), jnp.sum(dpre, axis=0), c * fw, axis=0
    ).reshape(ndev, -1)
    sums = [
        jnp.sum(dnorm1 * hat, axis=0).reshape(ndev, -1),
        jnp.sum(dnorm1, axis=0).reshape(ndev, -1),
        jnp.sum(dnorm2 * hat, axis=0).reshape(ndev, -1),
        jnp.sum(dnorm2, axis=0).reshape(ndev, -1),
        jnp.sum(g_ownf, axis=0).reshape(ndev, -1),
        sum_q,
        sum_u,
    ]
    sums = jnp.concatenate(sums, axis=1)
    sw = LANES * -(-sums.shape[1] // (piece * LANES))
    sums_pad = jnp.pad(sums, ((0, 0), (0, piece * sw - sums.shape[1]))).reshape(ndev * piece, sw)
    rows_out = tdot(ctx_c, g_all).astype(bf)
    wide = jnp.concatenate(
        [
            tdot(norm1, dqkv_b).astype(bf),
            tdot(norm2, dpre_b).astype(bf),
            tdot(g_all, hidden).astype(bf),
            sums_pad.astype(bf),
            rows_out.reshape(ndev * piece, -1),
        ],
        axis=1,
    )
    wide = lax.psum_scatter(wide, "fsdp", scatter_dimension=0, tiled=True)
    split = 3 * qw + 2 * fw + sw
    grad_wout = lax.ppermute(wide[:, split:].reshape(piece, dmodel), both, back).astype(f32)
    wide = lax.all_to_all(
        wide[:, :split].reshape(nctx, piece, split), "ctx", split_axis=0, concat_axis=0, tiled=True
    )
    sums = jnp.sum(wide[:, :, split - sw :].astype(f32), axis=0).reshape(-1)[: sums.shape[1]]
    wide = wide.transpose(1, 0, 2).astype(f32)
    grad_qkv = (
        wide[:, :, : 3 * qw].reshape(piece, nctx, 3, qw).transpose(0, 2, 1, 3).reshape(piece, -1)
    )
    grad_up = wide[:, :, 3 * qw : 3 * qw + fw].reshape(piece, ff)
    grad_down = wide[:, :, 3 * qw + fw : 3 * qw + 2 * fw].reshape(piece, ff)
    ends = [piece * i for i in range(6)] + [5 * piece + b_qkv.shape[0], sums.shape[0]]
    vs = [sums[a:b] for a, b in zip(ends[:-1], ends[1:])]
    return (
        layer_out,
        grad_x,
        vs[0],
        vs[1],
        vs[2],
        vs[3],
        grad_qkv,
        vs[5],
        grad_wout,
        vs[4],
        grad_up,
        vs[6],
        grad_down,
        vs[4],
    )


def solution(mesh):
    nctx = mesh.shape["ctx"]

    def pick(layer_in, *rest):
        heads = layer_in.shape[-1] // HD
        whole = heads % nctx == 0
        return (head_shards if whole else shards)(layer_in, *rest)

    return jax.shard_map(
        pick,
        mesh=mesh,
        in_specs=(
            P("ctx", "fsdp", None, None),
            P("ctx", "fsdp", None, None),
            P(),
            P(("fsdp", "ctx")),
            P(("fsdp", "ctx")),
            P(("fsdp", "ctx")),
            P(("fsdp", "ctx")),
            P(("fsdp", "ctx"), None),
            P(("fsdp", "ctx")),
            P(("fsdp", "ctx"), None),
            P(("fsdp", "ctx")),
            P(("fsdp", "ctx"), None),
            P(("fsdp", "ctx")),
            P(("fsdp", "ctx"), None),
            P(("fsdp", "ctx")),
        ),
        out_specs=(
            P("ctx", "fsdp", None, None),
            P("ctx", "fsdp", None, None),
            P(("fsdp", "ctx")),
            P(("fsdp", "ctx")),
            P(("fsdp", "ctx")),
            P(("fsdp", "ctx")),
            P(("fsdp", "ctx"), None),
            P(("fsdp", "ctx")),
            P(("fsdp", "ctx"), None),
            P(("fsdp", "ctx")),
            P(("fsdp", "ctx"), None),
            P(("fsdp", "ctx")),
            P(("fsdp", "ctx"), None),
            P(("fsdp", "ctx")),
        ),
        check_vma=False,
    )
```
